128 devices in a mesh: rows: 32 (over y_hi, z, x), cols: 4 (over y_lo, core).
Axes of the slice: x: 4, y: 4 (y_hi: 2, y_lo: 2; y = y_hi * 2 + y_lo), z: 4, core: 2. Of those that a mesh axis runs over, the one named last changes fastest.
Arguments:
- old_feats: bfloat16 [131072, 1024], P('rows'), may hold values from -6 to 6
- new_feats: bfloat16 [2048, 1024], P('cols', 'rows'), may hold values from -6 to 6
- factor_panel: float32 [131072, 1024], P('rows', 'cols'), as said below
- carried: float32 [131072, 2048], P('rows', 'cols'), may hold values from -4 to 4
- schur_in: float32 [2048, 2048], P('rows', 'cols'), may hold values from -6 to 6
- panel_index: int32 [1], replicated, may hold values from 0 to 131071
- owner_map: int32 [128], replicated, may hold values from 0 to 127, each once
Outputs:
- updated: float32 [131072, 2048], P('rows', 'cols')
- schur: float32 [2048, 2048], P('rows', 'cols')
The draws below stay inside these ranges and needn't reach their ends.
Inputs may be any that keep to these rules, and one draw needn't show every extreme that they name: panel_index names a logical training row. owner_map is a permutation of the row blocks; storage block s lies on index s // 4 of rows. `factor_panel`: within each block of 1024 rows, the lower triangle is a well-conditioned triangular factor.
All inputs are finite; a program needn't handle non-finite values.
Results may differ from the reference program's by a relative error of at most 0.0003.
Values may be sent and summed in bfloat16 or wider, within the bound.
A program may use at most 128 MiB of HBM per device.

```python
import math
import jax
import jax.numpy as jnp
from jax import lax

D = 1024
PANEL = 1024
NEW = 2048
NBLOCKS = 128
ROWS = 131072


def draw_factor_panel(key, part):
    key_off = jax.random.fold_in(key, 11)
    key_diag = jax.random.fold_in(key, 12)
    spread = 0.5 / math.sqrt(PANEL)
    off_diag = jax.random.normal(key_off, (ROWS, PANEL), jnp.float32) * spread
    diag_vals = jax.random.uniform(key_diag, (ROWS, 1), jnp.float32, 1.0, 2.0)
    local_row = jnp.arange(ROWS, dtype=jnp.int32) % PANEL
    on_diag = local_row[:, None] == jnp.arange(PANEL, dtype=jnp.int32)[None, :]
    return jnp.where(on_diag, diag_vals, off_diag).astype(jnp.float32)


def steps_of(rng, shape, shards, smallest, high):
    def one(position, shards_of):
        steps = jax.random.uniform(jax.random.fold_in(jax.random.fold_in(rng, 6), position), (shards_of,), jnp.float32, smallest / len(shards), high / len(shards))
        return jnp.repeat(jnp.exp(steps), shape[position] // shards_of).reshape((-1,) + (1,) * (len(shape) - position - 1))

    loudness = one(*shards[0])
    for cut in shards[1:]:
        loudness = loudness * one(*cut)
    return loudness


def noise(own_key, extent, scale, limit, cuts=(), kind=jnp.bfloat16):
    gain = steps_of(own_key, extent, cuts, -0.22, 0.18) if cuts else 1.0
    values = jax.random.normal(own_key, extent, jnp.float32) * scale * gain
    return jnp.minimum(jnp.maximum(values, -limit), limit).astype(kind)


def setup_inputs(seed: int = 0) -> dict:
    seeds = jax.random.split(jax.random.key(seed), 8)
    old_feats = noise(seeds[0], (ROWS, D), 1.0, 6.0, ((0, 32),))
    new_feats = noise(seeds[1], (NEW, D), 1.0, 6.0, ((0, 4), (1, 32)))
    factor_panel = draw_factor_panel(jax.random.fold_in(seeds[7], 71), 0)
    carried = noise(seeds[3], (ROWS, NEW), 0.5, 4.0, ((0, 32), (1, 4)), jnp.float32)
    schur_in = noise(seeds[4], (NEW, NEW), 1.0, 6.0, ((0, 32), (1, 4)), jnp.float32)
    panel_index = jax.random.randint(seeds[5], (1,), 0, ROWS).astype(jnp.int32)
    owner_map = jax.random.permutation(seeds[6], NBLOCKS).astype(jnp.int32)
    return dict(old_feats=old_feats, new_feats=new_feats, factor_panel=factor_panel, carried=carried, schur_in=schur_in, panel_index=panel_index, owner_map=owner_map)


def reference(old_feats, new_feats, factor_panel, carried, schur_in, panel_index, owner_map):
    dots = jnp.dot(old_feats.astype(jnp.float32), new_feats.astype(jnp.float32).T, precision=lax.Precision.HIGHEST) / math.sqrt(D)
    work = 0.25 * (1.0 + dots) ** 2 - carried
    panel = (panel_index[0] // PANEL).astype(jnp.int32)
    storage = owner_map[panel]
    logical = jnp.zeros((NBLOCKS,), jnp.int32).at[owner_map].set(jnp.arange(NBLOCKS, dtype=jnp.int32))
    start = (storage * PANEL).astype(jnp.int32)
    work_block = lax.dynamic_slice_in_dim(work, start, PANEL, 0)
    tri_block = jnp.tril(lax.dynamic_slice_in_dim(factor_panel, start, PANEL, 0))
    solved = lax.linalg.triangular_solve(tri_block, work_block, left_side=True, lower=True)
    update = jnp.dot(factor_panel, solved, precision=lax.Precision.HIGHEST)
    row_logical = jnp.repeat(logical, PANEL)
    result = jnp.where(row_logical[:, None] > panel, work - update, work)
    result = lax.dynamic_update_slice_in_dim(result, solved, start, 0)
    schur = schur_in - jnp.dot(solved.T, solved, precision=lax.Precision.HIGHEST) / PANEL
    return (result, schur)
```

```python
import jax
import jax.numpy as jnp
from jax import lax
from jax.experimental import pallas as pl
from jax.experimental.pallas import tpu as pltpu
from jax.sharding import PartitionSpec as P

MESH = pl.DeviceIdType.MESH
F32, BF16, I16, I32 = jnp.float32, jnp.bfloat16, jnp.int16, jnp.int32
ANY = pl.BlockSpec(memory_space=pl.ANY)

PANEL = 1024
BLOCKS = 4
COLS = 4
PLANE = 16
SLAB = PANEL // COLS
TILE = 512
EBIAS = 128


def encode(x):
    rows, lanes = x.shape
    g = x.reshape(rows // 8, 8, lanes)
    top = jnp.max(jnp.abs(g), axis=1, keepdims=True)
    e = jnp.ceil(jnp.log2(jnp.maximum(top, 1e-30) * (1.0 / 16383.0)))
    e = jnp.clip(e, -126.0, 126.0)
    k = jnp.round(g * jnp.exp2(-e))
    k = jnp.clip(k, -16383.0, 16383.0).astype(I32)
    place = lax.broadcasted_iota(I32, g.shape, 1)
    bit = ((e.astype(I32) + EBIAS) >> place) & 1
    return (k * 2 + bit).astype(I16).reshape(rows, lanes)


def decode(codes):
    rows, lanes = codes.shape
    v = codes.astype(I32).reshape(rows // 8, 8, lanes)
    place = lax.broadcasted_iota(I32, v.shape, 1)
    e = jnp.sum((v & 1) << place, axis=1, keepdims=True) - EBIAS
    return ((v >> 1).astype(F32) * jnp.exp2(e.astype(F32))).reshape(rows, lanes)


def split(x):
    hi = x.astype(BF16)
    return hi, (x - hi.astype(F32)).astype(BF16)


def mm(a, b):
    return jnp.dot(a, b, preferred_element_type=F32)


def mm3(ahi, alo, bhi, blo):
    return mm(ahi, bhi) + mm(alo, bhi) + mm(ahi, blo)


def position(pi, om):
    storage = om[pi[0] >> 10]
    return storage >> 2, storage & 3


def rolled(k, pi, om):
    return (position(pi, om)[1] + k) & 3


def encode_kernel(pi, om, p_ref, out_ref, m_ref, d_ref):
    k = pl.program_id(0)
    root, _ = position(pi, om)
    r, c = lax.axis_index("rows"), lax.axis_index("cols")

    def body(t, carry):
        rows = pl.ds(pl.multiple_of(t * 128, 128), 128)
        out_ref[0, rows, :] = encode(p_ref[rows, :])
        return carry

    lax.fori_loop(0, PANEL // 128, body, 0)

    @pl.when((k == 0) & (r == root))
    def _():
        rows = pl.ds(pl.multiple_of(c * SLAB, SLAB), SLAB)
        i = lax.broadcasted_iota(I32, (SLAB, SLAB), 0)
        j = lax.broadcasted_iota(I32, (SLAB, SLAB), 1)
        d = p_ref[rows, :]
        d_ref[...] = d
        m_ref[...] = jnp.where(i == j, 1.0 / jnp.where(i == j, d, 1.0), 0.0)

        def level(b, carry):
            below = ((i >> b) & 1 == 1) & ((j >> b) + 1 == (i >> b))
            m = m_ref[...]
            t = jnp.dot(
                jnp.where(below, d_ref[...], 0.0), m, precision=lax.Precision.HIGHEST,
                preferred_element_type=F32,
            )
            m_ref[...] = m - jnp.dot(
                m, t, precision=lax.Precision.HIGHEST, preferred_element_type=F32
            )
            return carry

        lax.fori_loop(0, SLAB.bit_length() - 1, level, 0)
        out_ref[0, rows, :] = encode(m_ref[...])


def encode_panel(pi, om, panel):
    return pl.pallas_call(
        encode_kernel,
        out_shape=jax.ShapeDtypeStruct((BLOCKS, PANEL, SLAB), I16),
        grid_spec=pltpu.PrefetchScalarGridSpec(
            num_scalar_prefetch=2,
            grid=(BLOCKS,),
            in_specs=[pl.BlockSpec((PANEL, SLAB), lambda k, pi, om: (rolled(k, pi, om), 0))],
            out_specs=pl.BlockSpec((1, PANEL, SLAB), lambda k, pi, om: (k, 0, 0)),
            scratch_shapes=[pltpu.VMEM((SLAB, SLAB), F32), pltpu.VMEM((SLAB, SLAB), F32)],
        ),
        name="encode_panel",
    )(pi, om, panel)


def greet(peers):
    barrier = pltpu.get_barrier_semaphore()
    for peer in peers:
        pl.semaphore_signal(barrier, inc=1, device_id=peer, device_id_type=MESH)
    pl.semaphore_wait(barrier, len(peers))


def send(src, dst, ssem, rsem, peer):
    copy = pltpu.make_async_remote_copy(
        src_ref=src, dst_ref=dst, send_sem=ssem, recv_sem=rsem, device_id=peer,
        device_id_type=MESH,
    )
    copy.start()
    return copy


def gather_kernel(f_ref, p_ref, all_ref, land_ref, own, fs, fr, ps, pr):
    r, c = lax.axis_index("rows"), lax.axis_index("cols")
    pieces = ps.shape[0]
    rows = PANEL // pieces
    greet([(r ^ d, c) for d in range(1, PLANE + 1)] + [(r, c ^ d) for d in (1, 2)])
    over = send(f_ref, all_ref.at[r], fs.at[0], fr.at[0], (r ^ PLANE, c))
    cross = []
    for t in range(pieces):
        part = pl.ds(t * rows, rows)
        cross.append(
            send(p_ref.at[0, part], land_ref.at[1, part], ps.at[t, 0], pr.at[t, 0], (r, c ^ 2))
        )
    firsts = [
        send(f_ref, all_ref.at[r], fs.at[d], fr.at[d], (r ^ d, c)) for d in range(1, PLANE)
    ]
    mine = pltpu.make_async_copy(f_ref, all_ref.at[r], own)
    mine.start()
    near = send(p_ref.at[0], land_ref.at[0], ps.at[0, 2], pr.at[0, 2], (r, c ^ 1))
    over.wait_recv()
    other = all_ref.at[r ^ PLANE]
    seconds = [
        send(other, other, fs.at[PLANE + d], fr.at[PLANE + d], (r ^ d, c))
        for d in range(1, PLANE)
    ]
    relays = []
    for t in range(pieces):
        part = pl.ds(t * rows, rows)
        cross[t].wait_recv()
        relays.append(
            send(land_ref.at[1, part], land_ref.at[2, part], ps.at[t, 1], pr.at[t, 1], (r, c ^ 1))
        )
    over.wait_send()
    mine.wait()
    near.wait()
    for copy in firsts + seconds + relays:
        copy.wait()
    for copy in cross:
        copy.wait_send()


def gather(feats, codes):
    pieces = 4
    return pl.pallas_call(
        gather_kernel,
        out_shape=(
            jax.ShapeDtypeStruct((2 * PLANE,) + feats.shape, BF16),
            jax.ShapeDtypeStruct((3, PANEL, SLAB), I16),
        ),
        in_specs=[ANY, ANY],
        out_specs=(ANY, ANY),
        scratch_shapes=[
            pltpu.SemaphoreType.DMA(()),
            pltpu.SemaphoreType.DMA((2 * PLANE,)),
            pltpu.SemaphoreType.DMA((2 * PLANE,)),
            pltpu.SemaphoreType.DMA((pieces, 3)),
            pltpu.SemaphoreType.DMA((pieces, 3)),
        ],
        compiler_params=pltpu.CompilerParams(collective_id=0, has_side_effects=True),
        name="gather",
    )(feats, codes)


def solve_kernel(pi, om, x_ref, car_ref, f_ref, own_ref, land_ref, out_ref, w, lhi, llo):
    root, _ = position(pi, om)
    r, c = lax.axis_index("rows"), lax.axis_index("cols")

    @pl.when(r != root)
    def _():
        out_ref[...] = jnp.zeros_like(out_ref)

    @pl.when(r == root)
    def _():
        for d in range(COLS):
            def unpack(t, carry, d=d):
                rows = pl.ds(pl.multiple_of(t * 128, 128), 128)
                codes = own_ref[0, rows, :] if d == 0 else land_ref[d - 1, rows, :]
                hi, lo = split(decode(codes))
                lhi[c ^ d, rows, :] = hi
                llo[c ^ d, rows, :] = lo
                return carry

            lax.fori_loop(0, PANEL // 128, unpack, 0)

        def form(t, carry):
            rows = pl.ds(pl.multiple_of(t * SLAB, SLAB), SLAB)
            dots = mm(x_ref[rows, :], f_ref[...])
            w[rows, :] = 0.25 * (1.0 + dots * (1.0 / 32.0)) ** 2 - car_ref[rows, :]
            return carry

        lax.fori_loop(0, COLS, form, 0)

        def column(j, carry):
            rows = pl.ds(pl.multiple_of(j * SLAB, SLAB), SLAB)
            whi, wlo = split(w[rows, :])
            x = mm3(lhi[j, rows, :], llo[j, rows, :], whi, wlo)
            w[rows, :] = x
            xhi, xlo = split(x)

            def below(i, carry):
                low = pl.ds(pl.multiple_of(i * SLAB, SLAB), SLAB)
                w[low, :] -= mm3(lhi[j, low, :], llo[j, low, :], xhi, xlo)
                return carry

            return lax.fori_loop(j + 1, COLS, below, carry)

        lax.fori_loop(0, COLS, column, 0)

        def pack(t, carry):
            rows = pl.ds(pl.multiple_of(t * 64, 64), 64)
            out_ref[t] = encode(w[rows, :])
            return carry

        lax.fori_loop(0, PLANE, pack, 0)


def solve(pi, om, old, carried, feats, codes, land):
    width, new = feats.shape
    return pl.pallas_call(
        solve_kernel,
        out_shape=jax.ShapeDtypeStruct((PLANE, PANEL // PLANE, new), I16),
        grid_spec=pltpu.PrefetchScalarGridSpec(
            num_scalar_prefetch=2,
            grid=(1,),
            in_specs=[
                pl.BlockSpec((PANEL, width), lambda k, pi, om: (rolled(0, pi, om), 0)),
                pl.BlockSpec((PANEL, new), lambda k, pi, om: (rolled(0, pi, om), 0)),
                pl.BlockSpec((width, new), lambda k, pi, om: (0, 0)),
                pl.BlockSpec((1, PANEL, SLAB), lambda k, pi, om: (0, 0, 0)),
                pl.BlockSpec((3, PANEL, SLAB), lambda k, pi, om: (0, 0, 0)),
            ],
            out_specs=pl.BlockSpec((PLANE, PANEL // PLANE, new), lambda k, pi, om: (0, 0, 0)),
            scratch_shapes=[
                pltpu.VMEM((PANEL, new), F32),
                pltpu.VMEM((COLS, PANEL, SLAB), BF16),
                pltpu.VMEM((COLS, PANEL, SLAB), BF16),
            ],
        ),
        name="panel_solve",
    )(pi, om, old, carried, feats, codes, land)


def spread_kernel(
    s_ref, p_ref, all_ref, land_ref, side_ref, rbuf, half, ybuf, total, own, rs, rr, ys, yr, gs, gr,
    ps, pr, hs, hr
):
    r, c = lax.axis_index("rows"), lax.axis_index("cols")
    me = r & (PLANE - 1)
    pieces = ps.shape[0]
    rows = (BLOCKS - 1) * PANEL // pieces
    per = PANEL // rows
    greet([(r ^ d, c) for d in range(1, PLANE + 1)] + [(r, c ^ d) for d in (1, 2, 3)])

    reduces = [
        send(s_ref.at[me ^ d], rbuf.at[d], rs.at[d], rr.at[d], (r ^ d, c)) for d in range(1, PLANE)
    ]
    mine = pltpu.make_async_copy(s_ref.at[me], rbuf.at[0], own.at[0])
    mine.start()

    def part(t):
        return t // per, pl.ds(t % per * rows, rows)

    cross, nears, relays = [], [], []
    for t in range(pieces):
        b, rng = part(t)
        cross.append(
            send(p_ref.at[b + 1, rng], land_ref.at[1, b, rng], ps.at[t, 0], pr.at[t, 0], (r, c ^ 2))
        )
        nears.append(
            send(p_ref.at[b + 1, rng], land_ref.at[0, b, rng], ps.at[t, 1], pr.at[t, 1], (r, c ^ 1))
        )
    mine.wait()
    for copy in reduces:
        copy.wait_recv()

    def add(d, acc):
        return acc + rbuf[d].astype(I32)

    partial = lax.fori_loop(1, PLANE, add, rbuf[0].astype(I32))
    half[...] = partial.astype(I16)
    over = send(half, ybuf, ys, yr, (r ^ PLANE, c))

    def relay(t):
        b, rng = part(t)
        cross[t].wait_recv()
        relays.append(
            send(
                land_ref.at[1, b, rng], land_ref.at[2, b, rng], ps.at[t, 2], pr.at[t, 2], (r, c ^ 1)
            )
        )

    over.wait_recv()
    total[...] = (half[...].astype(I32) + ybuf[...].astype(I32)).astype(I16)
    gathers = [
        send(total, all_ref.at[me], gs.at[d], gr.at[d], (r ^ d, c)) for d in range(1, PLANE)
    ]
    put = pltpu.make_async_copy(total, all_ref.at[me], own.at[1])
    put.start()
    for t in range(pieces):
        relay(t)
    put.wait()
    for copy in gathers:
        copy.wait_recv()

    giver = r >> 3
    strip = all_ref.at[:, :, pl.ds(pl.multiple_of(((r & 7) >> 1) * 128, 128), 128)]

    @pl.when(c == giver)
    def _():
        copies = [send(strip, side_ref, hs.at[d], hr, (r, c ^ d)) for d in (1, 2, 3)]
        for copy in copies:
            copy.wait_send()

    @pl.when(c != giver)
    def _():
        pltpu.make_async_remote_copy(
            src_ref=side_ref, dst_ref=side_ref, send_sem=hs.at[0], recv_sem=hr,
            device_id=(r, c ^ 1), device_id_type=MESH,
        ).wait_recv()

    over.wait_send()
    for copy in reduces + gathers + cross:
        copy.wait_send()
    for copy in nears + relays:
        copy.wait()


def spread(solved, codes):
    pieces = 6
    chunk = solved.shape[1:]
    return pl.pallas_call(
        spread_kernel,
        out_shape=(
            jax.ShapeDtypeStruct(solved.shape, I16),
            jax.ShapeDtypeStruct((3, BLOCKS - 1, PANEL, SLAB), I16),
            jax.ShapeDtypeStruct((PLANE, PANEL // PLANE, 128), I16),
        ),
        in_specs=[ANY, ANY],
        out_specs=(ANY, ANY, ANY),
        scratch_shapes=[
            pltpu.VMEM(solved.shape, I16),
            pltpu.VMEM(chunk, I16),
            pltpu.VMEM(chunk, I16),
            pltpu.VMEM(chunk, I16),
            pltpu.SemaphoreType.DMA((2,)),
            pltpu.SemaphoreType.DMA((PLANE,)),
            pltpu.SemaphoreType.DMA((PLANE,)),
            pltpu.SemaphoreType.DMA(()),
            pltpu.SemaphoreType.DMA(()),
            pltpu.SemaphoreType.DMA((PLANE,)),
            pltpu.SemaphoreType.DMA((PLANE,)),
            pltpu.SemaphoreType.DMA((pieces, 3)),
            pltpu.SemaphoreType.DMA((pieces, 3)),
            pltpu.SemaphoreType.DMA((4,)),
            pltpu.SemaphoreType.DMA(()),
        ],
        compiler_params=pltpu.CompilerParams(collective_id=1, has_side_effects=True),
        name="spread",
    )(solved, codes)


def update_kernel(
    pi, om, x_ref, car_ref, f_ref, own_ref, land0_ref, land_ref, s_ref, side_ref, schur_ref,
    out_ref, gram_ref, shi, slo, phi, plo, prod, order
):
    i = pl.program_id(0)
    root, slot = position(pi, om)
    panel = pi[0] >> 10
    r, c = lax.axis_index("rows"), lax.axis_index("cols")
    per = PANEL // TILE

    @pl.when(i == 0)
    def _():
        def find(b, carry):
            s = om[b]

            @pl.when((s >> 2) == r)
            def _():
                order[s & 3] = b

            return carry

        lax.fori_loop(0, om.shape[0], find, 0)

        def unpack(t, carry):
            rows = pl.ds(pl.multiple_of(t * 64, 64), 64)
            hi, lo = split(decode(s_ref[t]))
            shi[rows, :] = hi
            slo[rows, :] = lo
            return carry

        lax.fori_loop(0, PLANE, unpack, 0)
        giver = r >> 3
        lanes = pl.ds(pl.multiple_of(((r & 7) >> 1) * 128, 128), 128)

        def side(codes):
            hi, lo = split(decode(codes.reshape(PANEL, 128)))
            dims = (((0,), (0,)), ((), ()))

            def prods(a, b):
                return lax.dot_general(a, b[...], dims, preferred_element_type=F32)

            prod[...] = prods(hi, shi) + prods(lo, shi) + prods(hi, slo)

        @pl.when(c == giver)
        def _():
            side(s_ref[:, :, lanes])

        @pl.when(c != giver)
        def _():
            side(side_ref[...])

        gram = prod[pl.ds(pl.multiple_of((r & 1) * 64, 64), 64), :]
        gram_ref[...] = schur_ref[...] - gram * (1.0 / PANEL)

    k = i // per
    block = (slot + k) & 3
    held = (k == 0) & (r == root)
    above = order[block] > panel

    @pl.when(held)
    def _():
        rows = pl.ds(pl.multiple_of(i % per * TILE, TILE), TILE)
        out_ref[...] = shi[rows, :].astype(F32) + slo[rows, :].astype(F32)

    @pl.when(jnp.logical_not(held))
    def _():
        dots = mm(x_ref[...], f_ref[...])
        out_ref[...] = 0.25 * (1.0 + dots * (1.0 / 32.0)) ** 2 - car_ref[...]

    @pl.when(above & jnp.logical_not(held))
    def _():
        def unpack(ref, lead, d):
            def body(t, carry):
                rows = pl.ds(pl.multiple_of(t * 64, 64), 64)
                hi, lo = split(decode(ref[lead + (rows, slice(None))]))
                phi[d, rows, :] = hi
                plo[d, rows, :] = lo
                return carry

            lax.fori_loop(0, TILE // 64, body, 0)

        unpack(own_ref, (0,), 0)
        for d in range(1, COLS):
            @pl.when(k == 0)
            def _():
                unpack(land0_ref, (d - 1,), d)

            @pl.when(k > 0)
            def _():
                unpack(land_ref, (d - 1, 0), d)

        acc = None
        for d in range(COLS):
            rows = pl.ds(pl.multiple_of((c ^ d) * SLAB, SLAB), SLAB)
            term = mm3(phi[d], plo[d], shi[rows, :], slo[rows, :])
            acc = term if acc is None else acc + term
        out_ref[...] -= acc


def update(pi, om, old, carried, feats, codes, land0, land, solved, side, schur_in):
    rows, width = old.shape
    new = feats.shape[1]
    per = PANEL // TILE

    def tile(i, pi, om):
        return rolled(i // per, pi, om) * per + i % per, 0

    return pl.pallas_call(
        update_kernel,
        out_shape=(
            jax.ShapeDtypeStruct((rows, new), F32),
            jax.ShapeDtypeStruct(schur_in.shape, F32),
        ),
        grid_spec=pltpu.PrefetchScalarGridSpec(
            num_scalar_prefetch=2,
            grid=(rows // TILE,),
            in_specs=[
                pl.BlockSpec((TILE, width), tile),
                pl.BlockSpec((TILE, new), tile),
                pl.BlockSpec((width, new), lambda i, pi, om: (0, 0)),
                pl.BlockSpec((1, TILE, SLAB), lambda i, pi, om: (i // per, i % per, 0)),
                pl.BlockSpec((3, TILE, SLAB), lambda i, pi, om: (0, jnp.minimum(i, per - 1), 0)),
                pl.BlockSpec(
                    (3, 1, TILE, SLAB),
                    lambda i, pi, om: (
                        0, jnp.maximum(i // per - 1, 0), jnp.where(i < per, 0, i % per), 0
                    ),
                ),
                pl.BlockSpec(solved.shape, lambda i, pi, om: (0, 0, 0)),
                pl.BlockSpec(side.shape, lambda i, pi, om: (0, 0, 0)),
                pl.BlockSpec(schur_in.shape, lambda i, pi, om: (0, 0)),
            ],
            out_specs=(
                pl.BlockSpec((TILE, new), tile),
                pl.BlockSpec(schur_in.shape, lambda i, pi, om: (0, 0)),
            ),
            scratch_shapes=[
                pltpu.VMEM((PANEL, new), BF16),
                pltpu.VMEM((PANEL, new), BF16),
                pltpu.VMEM((COLS, TILE, SLAB), BF16),
                pltpu.VMEM((COLS, TILE, SLAB), BF16),
                pltpu.VMEM((128, new), F32),
                pltpu.SMEM((BLOCKS,), I32),
            ],
        ),
        name="update",
    )(pi, om, old, carried, feats, codes, land0, land, solved, side, schur_in)


def local(old_feats, new_feats, factor_panel, carried, schur_in, panel_index, owner_map):
    pi, om = panel_index, owner_map
    codes = encode_panel(pi, om, factor_panel)
    feats, land0 = gather(new_feats.T, codes)
    feats = feats.reshape(old_feats.shape[1], new_feats.shape[0])
    mine = solve(pi, om, old_feats, carried, feats, codes, land0)
    solved, land, side = spread(mine, codes)
    return update(
        pi, om, old_feats, carried, feats, codes, land0, land, solved, side, schur_in
    )


def solution(mesh):
    placed = (
        P("rows", None),
        P("cols", "rows"),
        P("rows", "cols"),
        P("rows", "cols"),
        P("rows", "cols"),
        P(),
        P(),
    )
    return jax.shard_map(
        local,
        mesh=mesh,
        in_specs=placed,
        out_specs=(P("rows", "cols"), P("rows", "cols")),
        check_vma=False,
    )
```

```python
import jax
import jax.numpy as jnp
from jax import lax
from jax.experimental import pallas as pl
from jax.experimental.pallas import tpu as pltpu
from jax.sharding import PartitionSpec as P

MESH = pl.DeviceIdType.MESH
F32, BF16, I16, I32 = jnp.float32, jnp.bfloat16, jnp.int16, jnp.int32
ANY = pl.BlockSpec(memory_space=pl.ANY)

PANEL = 1024
BLOCKS = 4
COLS = 4
SLAB = PANEL // COLS
PLANE = 16
BAND = 32
HALF = PANEL // 2
SUB = SLAB // 2
TILE = 512
EBIAS = 128


def encode(x, keep=1):
    rows, lanes = x.shape
    g = x.reshape(rows // 8, 8, lanes)
    top = jnp.max(jnp.abs(g), axis=1, keepdims=True)
    e = jnp.ceil(jnp.log2(jnp.maximum(top, 1e-30) * (1.0 / 16383.0)))
    e = jnp.clip(e, -126.0, 126.0)
    k = jnp.round(g * jnp.exp2(-e))
    k = jnp.clip(k, -16383.0, 16383.0).astype(I32)
    place = lax.broadcasted_iota(I32, g.shape, 1)
    bit = ((e.astype(I32) + EBIAS) >> place) & 1
    return ((k * 2 + bit) * keep).astype(I16).reshape(rows, lanes)


def decode(codes):
    rows, lanes = codes.shape
    v = codes.astype(I32).reshape(rows // 8, 8, lanes)
    place = lax.broadcasted_iota(I32, v.shape, 1)
    e = jnp.sum((v & 1) << place, axis=1, keepdims=True) - EBIAS
    return ((v >> 1).astype(F32) * jnp.exp2(e.astype(F32))).reshape(rows, lanes)


def split(x):
    hi = x.astype(BF16)
    return hi, (x - hi.astype(F32)).astype(BF16)


def mm(a, b):
    return jnp.dot(a, b, preferred_element_type=F32)


def mm3(ahi, alo, bhi, blo):
    return mm(ahi, bhi) + mm(alo, bhi) + mm(ahi, blo)


def position(pi, om):
    storage = om[pi[0] >> 10]
    return storage >> 2, storage & 3


def rolled(k, pi, om):
    return (position(pi, om)[1] + k) & 3


def kernel_columns(x, feats, carried):
    return 0.25 * (1.0 + mm(x, feats) * (1.0 / 32.0)) ** 2 - carried


def pick_block(ref, which, rows):
    out = ref[rows, :].astype(F32)
    named = jnp.full(out.shape, which, I32)
    for s in range(1, BLOCKS):
        other = ref[aligned(s * PANEL + rows.start, rows.size), :].astype(F32)
        out = jnp.where(named == s, other, out)
    return out


def aligned(start, size):
    return pl.ds(pl.multiple_of(start, size), size)


def times(a, b):
    return mm3(*split(a), *split(b))


def greet(peers):
    barrier = pltpu.get_barrier_semaphore()
    for peer in peers:
        pl.semaphore_signal(barrier, inc=1, device_id=peer, device_id_type=MESH)
    pl.semaphore_wait(barrier, len(peers))


def send(src, dst, sems, at, peer):
    copy = pltpu.make_async_remote_copy(
        src_ref=src, dst_ref=dst, send_sem=sems.at[(0,) + at], recv_sem=sems.at[(1,) + at],
        device_id=peer, device_id_type=MESH,
    )
    copy.start()
    return copy


def fetch(src, dst, sem):
    copy = pltpu.make_async_copy(src, dst, sem)
    copy.start()
    return copy


def panel_kernel(
    pi, om, new_ref, panel_ref, old_ref, car_ref,
    work_ref, codes_ref, land_ref, all_ref, side_ref,
    panel, old, work, feats, codes, lands, lhi, llo, w, diag, inv, mine, got1, sum1, got2, sum2,
    got3, sum3, local, fsem, bsem, s1, s2, s3, g1, g2, hsem,
):
    r, c = lax.axis_index("rows"), lax.axis_index("cols")
    x, z = r & 3, (r >> 2) & 3
    root, slot = position(pi, om)
    keep = (r == root).astype(I32)
    steps = (1, 2, 3)

    def on_x(d):
        return (r ^ d, c)

    def on_z(d):
        return (r ^ (d << 2), c)

    loads = [
        fetch(panel_ref, panel, local.at[0]),
        fetch(old_ref, old, local.at[1]),
        fetch(car_ref, work, local.at[2]),
        fetch(new_ref, feats.at[r], local.at[3]),
    ]
    greet([(r ^ d, c) for d in range(1, PLANE + 1)] + [(r, c ^ d) for d in steps])
    sent = []

    hop = send(new_ref, feats.at[r], fsem, (0,), (r ^ PLANE, c))
    order = (1, 4, 3, 12, 5, 15, 7, 13, 2, 8, 6, 9, 11, 14, 10)
    spreads = [send(new_ref, feats.at[r], fsem, (d,), (r ^ d, c)) for d in order]

    cross = []

    def dest(slab, k, rows):
        return lands.at[slab, rows] if k == 0 else land_ref.at[slab, k, rows]

    def ship(k, start, size, at):
        rows = aligned(start, size)
        cross.append(send(codes.at[k, rows], dest(1, k, rows), bsem, (at, 0), (r, c ^ 2)))
        sent.append(send(codes.at[k, rows], dest(0, k, rows), bsem, (at, 1), (r, c ^ 1)))

    relays = []

    def relay(k, start, size, at):
        rows = aligned(start, size)
        cross[at].wait_recv()
        relays.append(send(dest(1, k, rows), dest(2, k, rows), bsem, (at, 2), (r, c ^ 1)))

    def pack_rows(k, start, count):
        which = (slot + k) & 3

        def body(t, carry):
            rows = aligned(start + t * 64, 64)
            codes[k, rows, :] = encode(pick_block(panel, which, rows))
            return carry

        lax.fori_loop(0, count // 64, body, 0)

    loads[0].wait()
    for u in steps:
        start = ((c + u) & 3) * SLAB
        pack_rows(0, start, SLAB)
        ship(0, start, SLAB, u - 1)
    hop.wait_recv()
    other = feats.at[r ^ PLANE]
    spreads += [send(other, other, fsem, (PLANE + d,), (r ^ d, c)) for d in order]

    diag[...] = pick_block(panel, slot, aligned(c * SLAB, SLAB))
    i = lax.broadcasted_iota(I32, (SUB, SUB), 0)
    j = lax.broadcasted_iota(I32, (SUB, SUB), 1)
    corners = [pl.ds(q * SUB, SUB) for q in range(2)]
    inv[...] = jnp.zeros_like(inv)
    for q in corners:
        inv[q, q] = jnp.where(i == j, 1.0 / jnp.where(i == j, diag[q, q], 1.0), 0.0)

    def level(b, carry):
        below = ((i >> b) & 1 == 1) & ((j >> b) + 1 == (i >> b))
        for q in corners:
            m = inv[q, q]
            inv[q, q] = m - times(m, times(jnp.where(below, diag[q, q], 0.0), m))
        return carry

    lax.fori_loop(0, SUB.bit_length() - 1, level, 0)
    low, high = corners
    inv[high, low] = -times(inv[high, high], times(diag[high, low], inv[low, low]))

    def pick(t, carry):
        rows = aligned(t * 64, 64)
        held = jnp.full((64, SLAB), keep, I32) == 1
        codes[0, aligned(c * SLAB + t * 64, 64), :] = encode(
            jnp.where(held, inv[rows, :], diag[rows, :])
        )
        return carry

    lax.fori_loop(0, SLAB // 64, pick, 0)
    ship(0, c * SLAB, SLAB, COLS - 1)

    chunks = [(k, h * HALF, HALF, COLS + 2 * (k - 1) + h) for k in range(1, BLOCKS) for h in (0, 1)]
    for k, start, size, at in chunks:
        pack_rows(k, start, size)
        ship(k, start, size, at)
    puts = [fetch(codes, codes_ref, local.at[4])]
    for u in range(1, COLS + 1):
        relay(0, (((c ^ 2) + u) & 3) * SLAB, SLAB, u - 1)
    for near in sent[:COLS]:
        near.wait_recv()
    for far in relays[:COLS]:
        far.wait_recv()
    puts.append(fetch(lands, land_ref.at[:, 0], local.at[5]))

    for d in range(COLS):
        def unpack(t, carry, d=d):
            rows = aligned(t * 64, 64)
            piece = codes[0, rows, :] if d == 0 else lands[d - 1, rows, :]
            hi, lo = split(decode(piece))
            lhi[c ^ d, rows, :] = hi
            llo[c ^ d, rows, :] = lo
            return carry

        lax.fori_loop(0, PANEL // 64, unpack, 0)

    for copy in loads[1:]:
        copy.wait()
    for copy in spreads:
        copy.wait_recv()

    def columns(rows, carry):
        return kernel_columns(rows, feats[...].reshape(-1, feats.shape[2]), carry)

    def form(t, carry):
        rows = aligned(t * SLAB, SLAB)
        w[rows, :] = columns(
            pick_block(old, slot, rows).astype(BF16), pick_block(work, slot, rows)
        )
        return carry

    lax.fori_loop(0, COLS, form, 0)

    def column(j, carry):
        rows = aligned(j * SLAB, SLAB)
        solved = mm3(lhi[j, rows, :], llo[j, rows, :], *split(w[rows, :]))
        w[rows, :] = solved
        shi, slo = split(solved)

        def below(i, carry):
            under = aligned(i * SLAB, SLAB)
            w[under, :] -= mm3(lhi[j, under, :], llo[j, under, :], shi, slo)
            return carry

        return lax.fori_loop(j + 1, COLS, below, carry)

    lax.fori_loop(0, COLS, column, 0)

    def pack(t, carry):
        mine[t] = encode(w[aligned(t * BAND, BAND), :], keep)
        return carry

    lax.fori_loop(0, PANEL // BAND, pack, 0)

    def fill(start, stop):
        def body(t, carry):
            rows = aligned(t * SLAB, SLAB)
            work[rows, :] = columns(old[rows, :], work[rows, :])
            return carry

        lax.fori_loop(start, stop, body, 0)

    def quarter(h, a):
        return pl.ds(h * PLANE + a * 4, 4)

    def total(own, others):
        acc = own.astype(I32)
        for d in steps:
            acc = acc + others[d - 1].astype(I32)
        return acc.astype(I16)

    out1 = []
    for d in steps:
        out1.append(send(mine.at[quarter(0, x ^ d)], got1.at[0, d - 1], s1, (0, d), on_x(d)))
        out1.append(send(mine.at[quarter(1, z ^ d)], got1.at[1, d - 1], s1, (1, d), on_z(d)))
    for chunk in chunks[:2]:
        relay(*chunk)
    fill(0, 8)
    for copy in out1:
        copy.wait_recv()
    for h, a in ((0, x), (1, z)):
        sum1[h] = total(mine[quarter(h, a)], [got1[h, d - 1] for d in steps])
    out2 = []
    for d in steps:
        out2.append(send(sum1.at[0, z ^ d], got2.at[0, d - 1], s2, (0, d), on_z(d)))
        out2.append(send(sum1.at[1, x ^ d], got2.at[1, d - 1], s2, (1, d), on_x(d)))
    for chunk in chunks[2:4]:
        relay(*chunk)
    fill(8, 12)
    for copy in out2:
        copy.wait_recv()
    for h, a in ((0, z), (1, x)):
        sum2[h] = total(sum1[h, a], [got2[h, d - 1] for d in steps])
    swap = send(sum2, got3, s3, (), (r ^ PLANE, c))
    fill(12, 16)
    puts.append(fetch(work, work_ref, local.at[6]))
    swap.wait_recv()
    sum3[...] = (sum2[...].astype(I32) + got3[...].astype(I32)).astype(I16)
    spot = (x * 4 + z, PLANE + z * 4 + x)
    seats = [fetch(sum3.at[h], all_ref.at[spot[h]], local.at[7 + h]) for h in (0, 1)]
    back1 = []
    for d in steps:
        back1.append(send(sum3.at[0], all_ref.at[spot[0]], g1, (0, d), on_z(d)))
        back1.append(send(sum3.at[1], all_ref.at[spot[1]], g1, (1, d), on_x(d)))
    for chunk in chunks[4:]:
        relay(*chunk)
    for copy in seats:
        copy.wait()
    for copy in back1:
        copy.wait_recv()
    back2 = []
    for d in steps:
        for h, a, peer in ((0, x, on_x(d)), (1, z, on_z(d))):
            part = all_ref.at[quarter(h, a)]
            back2.append(send(part, part, g2, (h, d), peer))

    giver = r >> 3
    lanes = pl.ds(pl.multiple_of(((r & 7) >> 1) * 128, 128), 128)

    def strip(at, part, d):
        return pltpu.make_async_remote_copy(
            src_ref=all_ref.at[part, :, lanes], dst_ref=side_ref.at[part],
            send_sem=hsem.at[0, at, d], recv_sem=hsem.at[1, at, 0], device_id=(r, c ^ d),
            device_id_type=MESH,
        )

    parts = [quarter(0, x), quarter(1, z)]

    def give(at):
        @pl.when(c == giver)
        def _():
            for d in steps:
                strip(at, parts[at], d).start()

    give(0)
    give(1)
    for at, copy in enumerate(back2):
        copy.wait_recv()
        d, h = at // 2 + 1, at % 2
        parts.append(quarter(h, (z if h else x) ^ d))
        give(at + 2)

    @pl.when(c == giver)
    def _():
        for at, part in enumerate(parts):
            for d in steps:
                strip(at, part, d).wait_send()

    @pl.when(c != giver)
    def _():
        for at, part in enumerate(parts):
            strip(at, part, 1).wait_recv()

    for near in sent[COLS:]:
        near.wait_recv()
    for far in relays[COLS:]:
        far.wait_recv()
    for copy in [hop, swap] + spreads + sent + cross + relays + out1 + out2 + back1 + back2:
        copy.wait_send()
    for copy in puts:
        copy.wait()


def panel_steps(pi, om, new, panel, old, carried):
    rows, count = carried.shape
    bands = (PANEL // BAND, BAND, count)
    pair = (2, BAND, count)
    sems = pltpu.SemaphoreType.DMA
    smem = pl.BlockSpec(memory_space=pltpu.SMEM)
    return pl.pallas_call(
        panel_kernel,
        out_shape=(
            jax.ShapeDtypeStruct((rows, count), F32),
            jax.ShapeDtypeStruct((BLOCKS, PANEL, SLAB), I16),
            jax.ShapeDtypeStruct((3, BLOCKS, PANEL, SLAB), I16),
            jax.ShapeDtypeStruct(bands, I16),
            jax.ShapeDtypeStruct(bands[:2] + (128,), I16),
        ),
        in_specs=[smem, smem, ANY, ANY, ANY, ANY],
        out_specs=(ANY,) * 5,
        scratch_shapes=[
            pltpu.VMEM(panel.shape, F32),
            pltpu.VMEM(old.shape, BF16),
            pltpu.VMEM((rows, count), F32),
            pltpu.VMEM((2 * PLANE,) + new.shape, BF16),
            pltpu.VMEM((BLOCKS, PANEL, SLAB), I16),
            pltpu.VMEM((3, PANEL, SLAB), I16),
            pltpu.VMEM((COLS, PANEL, SLAB), BF16),
            pltpu.VMEM((COLS, PANEL, SLAB), BF16),
            pltpu.VMEM((PANEL, count), F32),
            pltpu.VMEM((SLAB, SLAB), F32),
            pltpu.VMEM((SLAB, SLAB), F32),
            pltpu.VMEM(bands, I16),
            pltpu.VMEM((2, 3, 4, BAND, count), I16),
            pltpu.VMEM((2, 4, BAND, count), I16),
            pltpu.VMEM((2, 3, BAND, count), I16),
            pltpu.VMEM(pair, I16),
            pltpu.VMEM(pair, I16),
            pltpu.VMEM(pair, I16),
            sems((9,)),
            sems((2, 2 * PLANE)),
            sems((2, 10, 3)),
            sems((2, 2, 4)),
            sems((2, 2, 4)),
            sems((2,)),
            sems((2, 2, 4)),
            sems((2, 2, 4)),
            sems((2, 8, 4)),
        ],
        compiler_params=pltpu.CompilerParams(collective_id=0, has_side_effects=True),
        name="panel_steps",
    )(pi, om, new, panel, old, carried)


def update_kernel(
    pi, om, work_ref, own_ref, land_ref, s_ref, side_ref, schur_ref,
    out_ref, gram_ref, right, rlow, left, thi, tlo, prod, order
):
    i = pl.program_id(0)
    root, slot = position(pi, om)
    panel = pi[0] >> 10
    r, c = lax.axis_index("rows"), lax.axis_index("cols")
    per = PANEL // TILE

    @pl.when(i == 0)
    def _():
        def find(b, carry):
            s = om[b]

            @pl.when((s >> 2) == r)
            def _():
                order[s & 3] = b

            return carry

        lax.fori_loop(0, om.shape[0], find, 0)

        def place(t):
            group = t * BAND // SLAB
            return (group ^ c) * SLAB + (t * BAND) % SLAB

        def unpack(t, carry):
            hi, lo = split(decode(s_ref[t]))
            right[aligned(place(t), BAND), :] = hi
            right[aligned(PANEL + place(t), BAND), :] = hi
            rlow[aligned(place(t), BAND), :] = lo
            return carry

        lax.fori_loop(0, PANEL // BAND, unpack, 0)
        lanes = pl.ds(pl.multiple_of(((r & 7) >> 1) * 128, 128), 128)

        def side(read):
            def body(t, carry):
                hi, lo = split(decode(read(t)))
                thi[aligned(place(t), BAND), :] = hi
                tlo[aligned(place(t), BAND), :] = lo
                return carry

            lax.fori_loop(0, PANEL // BAND, body, 0)

        @pl.when(c == r >> 3)
        def _():
            side(lambda t: s_ref[t, :, lanes])

        @pl.when(c != r >> 3)
        def _():
            side(lambda t: side_ref[t])

        def across(a, b):
            return lax.dot_general(a, b, (((0,), (0,)), ((), ())), preferred_element_type=F32)

        high = right[:PANEL, :]
        prod[...] = across(thi[...], high) + across(tlo[...], high) + across(thi[...], rlow[...])
        gram = prod[pl.ds(pl.multiple_of((r & 1) * 64, 64), 64), :]
        gram_ref[...] = schur_ref[...] - gram * (1.0 / PANEL)

    k = i // per
    held = (k == 0) & (r == root)
    above = order[(slot + k) & 3] > panel

    @pl.when(held)
    def _():
        def body(t, carry):
            out_ref[aligned(t * BAND, BAND), :] = decode(s_ref[i % per * (TILE // BAND) + t])
            return carry

        lax.fori_loop(0, TILE // BAND, body, 0)

    @pl.when(jnp.logical_not(held | above))
    def _():
        out_ref[...] = work_ref[...]

    @pl.when(above & jnp.logical_not(held))
    def _():
        for d in range(COLS):
            def body(t, carry, d=d):
                rows = aligned(t * 64, 64)
                piece = own_ref[0, rows, :] if d == 0 else land_ref[d - 1, 0, rows, :]
                hi, lo = split(decode(piece))
                left[rows, d * SLAB:(d + 1) * SLAB] = hi
                left[rows, PANEL + d * SLAB:PANEL + (d + 1) * SLAB] = lo
                return carry

            lax.fori_loop(0, TILE // 64, body, 0)
        out_ref[...] = work_ref[...] - mm(left[...], right[...]) - mm(left[:, :PANEL], rlow[...])


def update(pi, om, work, codes, land, solved, side, schur_in):
    rows, count = work.shape
    per = PANEL // TILE

    def tile(i, pi, om):
        return rolled(i // per, pi, om) * per + i % per, 0

    def whole(shape):
        return pl.BlockSpec(shape, lambda i, pi, om: (0,) * len(shape))

    return pl.pallas_call(
        update_kernel,
        out_shape=(
            jax.ShapeDtypeStruct((rows, count), F32),
            jax.ShapeDtypeStruct(schur_in.shape, F32),
        ),
        grid_spec=pltpu.PrefetchScalarGridSpec(
            num_scalar_prefetch=2,
            grid=(rows // TILE,),
            in_specs=[
                pl.BlockSpec((TILE, count), tile),
                pl.BlockSpec((1, TILE, SLAB), lambda i, pi, om: (i // per, i % per, 0)),
                pl.BlockSpec((3, 1, TILE, SLAB), lambda i, pi, om: (0, i // per, i % per, 0)),
                whole(solved.shape),
                whole(side.shape),
                whole(schur_in.shape),
            ],
            out_specs=(pl.BlockSpec((TILE, count), tile), whole(schur_in.shape)),
            scratch_shapes=[
                pltpu.VMEM((2 * PANEL, count), BF16),
                pltpu.VMEM((PANEL, count), BF16),
                pltpu.VMEM((TILE, 2 * PANEL), BF16),
                pltpu.VMEM((PANEL, 128), BF16),
                pltpu.VMEM((PANEL, 128), BF16),
                pltpu.VMEM((128, count), F32),
                pltpu.SMEM((BLOCKS,), I32),
            ],
        ),
        name="update",
    )(pi, om, work, codes, land, solved, side, schur_in)


def local(old_feats, new_feats, factor_panel, carried, schur_in, panel_index, owner_map):
    pi, om = panel_index, owner_map
    work, codes, land, solved, side = panel_steps(
        pi, om, new_feats.T, factor_panel, old_feats, carried
    )
    return update(pi, om, work, codes, land, solved, side, schur_in)


def solution(mesh):
    placed = (
        P("rows", None),
        P("cols", "rows"),
        P("rows", "cols"),
        P("rows", "cols"),
        P("rows", "cols"),
        P(),
        P(),
    )
    return jax.shard_map(
        local,
        mesh=mesh,
        in_specs=placed,
        out_specs=(P("rows", "cols"), P("rows", "cols")),
        check_vma=False,
    )
```
